32 devices in a mesh: grp: 2 (over y), band: 4 (over z), strm: 4 (over x, core).
Axes of the slice: x: 2, y: 2, z: 4, core: 2. Of those that a mesh axis runs over, the one named last changes fastest.
Arguments:
- latents: bfloat16 [8, 2, 4, 16, 384], P(('grp', 'strm'), None, 'band'), parts along dimension 0, may hold values from -6 to 6
- cache_first: bfloat16 [8, 2, 4, 16, 384], P(('grp', 'strm'), None, 'band'), parts along dimension 0, may hold values from -6 to 6
- cache_second: bfloat16 [8, 2, 8, 32, 192], P(('grp', 'strm'), None, 'band'), parts along dimension 0, may hold values from -6 to 6
- gain_first: float32 [384], replicated, may hold values from 0.25 to 1.75
- gain_second: float32 [192], replicated, may hold values from 0.25 to 1.75
- w_first: bfloat16 [3, 3, 3, 384, 768], P(None, None, None, None, 'strm'), may hold values from -0.0625 to 0.0625
- w_second: bfloat16 [3, 3, 3, 192, 192], P(None, None, None, None, 'strm'), may hold values from -0.078125 to 0.078125
- cache_slot: int32 [8], P('grp'), parts along dimension 0, may hold values from 0 to 3, as said below
- block_index: int32 [8], P('grp'), parts along dimension 0, may hold values from 0 to 3, as said below
Outputs:
- decoded: bfloat16 [8, 2, 8, 32, 192], P(('grp', 'strm'), None, 'band'), parts along dimension 0
The draws below stay inside these ranges and needn't reach their ends.
There are 2 independent parts, one for each index of `grp`. The reference program is written for one: setup_inputs(seed, part) draws one part's arguments, and reference() takes and returns one part's arrays. A program takes and returns all parts, laid end to end along the dimension named above; an argument that names none is the same for every part. Nothing has to cross between parts.
Inputs may be any that keep to these rules, and one draw needn't show every extreme that they name: `cache_slot`: each slot holds the caches of exactly one stream. The caches are read only where block_index > 0; exactly one stream of a group has block number 0.
All inputs are finite; a program needn't handle non-finite values.
Results may differ from the reference program's by a relative error of at most 0.0056.
Values may be sent and summed in bfloat16 or wider, within the bound.
A program may use at most 64 MiB of HBM per device.

```python
import jax
import jax.numpy as jnp
from jax import lax

C_IN = 384
C_OUT = 192
FRAMES = 2
COLS = 16
STREAMS = 4
HEIGHT = 4


def draw_cache_slot(key, part):
    return jax.random.permutation(jax.random.fold_in(key, 11), STREAMS).astype(jnp.int32)


def draw_block_index(key, part):
    inner = jax.random.fold_in(key, 23)
    values = jax.random.randint(jax.random.fold_in(inner, 1), (STREAMS,), 1, 4).astype(jnp.int32)
    fresh = jax.random.randint(jax.random.fold_in(inner, 2), (), 0, STREAMS).astype(jnp.int32)
    positions = jnp.arange(STREAMS, dtype=jnp.int32)
    return jnp.where(positions == fresh, jnp.zeros_like(values), values).astype(jnp.int32)


def block_scale(key, extent, split, least, largest):
    factor_of, own = 1.0, jax.random.fold_in(key, 6)
    for position, shards_of in split:
        steps = jnp.exp(jax.random.uniform(jax.random.fold_in(own, position), (shards_of,), jnp.float32, least / len(split), largest / len(split)))
        factor_of = factor_of * jnp.repeat(steps, extent[position] // shards_of).reshape([-1 if axis == position else 1 for axis in range(len(extent))])
    return factor_of


def gaussian(stream_key, shape, scale, bound, pieces=(), kind=jnp.bfloat16):
    factor_of = block_scale(stream_key, shape, pieces, -0.22, 0.18) if pieces else 1.0
    drawn = jax.random.normal(stream_key, shape, jnp.float32) * scale * factor_of
    return jnp.minimum(jnp.maximum(drawn, -bound), bound).astype(kind)


def setup_inputs(seed: int = 0, part: int = 0) -> dict:
    arg_keys = jax.random.split(jax.random.key(seed), 10)
    own_keys = jax.random.split(jax.random.fold_in(arg_keys[9], part), 10)
    return {
        "latents": gaussian(own_keys[0], (STREAMS, FRAMES, HEIGHT, COLS, C_IN), 1.0, 6.0, ((0, 4), (2, 4))),
        "cache_first": gaussian(own_keys[1], (STREAMS, 2, HEIGHT, COLS, C_IN), 1.0, 6.0, ((0, 4), (2, 4))),
        "cache_second": gaussian(own_keys[2], (STREAMS, 2, 2 * HEIGHT, 2 * COLS, C_OUT), 1.0, 6.0, ((0, 4), (2, 4))),
        "gain_first": jnp.clip(1.0 + 0.15 * jax.random.normal(arg_keys[3], (C_IN,), jnp.float32), 0.25, 1.75),
        "gain_second": jnp.clip(1.0 + 0.15 * jax.random.normal(arg_keys[4], (C_OUT,), jnp.float32), 0.25, 1.75),
        "w_first": gaussian(arg_keys[5], (3, 3, 3, C_IN, 4 * C_OUT), (27 * C_IN) ** -0.5, 0.0625, ((4, 4),)),
        "w_second": gaussian(arg_keys[6], (3, 3, 3, C_OUT, C_OUT), (27 * C_OUT) ** -0.5, 0.078125, ((4, 4),)),
        "cache_slot": draw_cache_slot(jax.random.fold_in(jax.random.fold_in(arg_keys[9], part), 71), part),
        "block_index": draw_block_index(jax.random.fold_in(jax.random.fold_in(arg_keys[9], part), 71), part),
    }


epsilon = 1e-06

def norm_silu(values, gain):
    mean_square = lax.optimization_barrier(jnp.mean(values * values, axis=-1, keepdims=True))
    return jax.nn.silu(values * lax.rsqrt(mean_square + epsilon) * gain.astype(jnp.float32))

def causal_conv(inputs, weight):
    padded = jnp.pad(inputs, ((0, 0), (0, 0), (0, 0), (1, 1), (0, 0)))
    count, span, height, width, channels = padded.shape
    frames = span - 2
    rows = height - 2
    columns = width - 2
    outputs = weight.shape[-1]
    summed = jnp.zeros((count * frames * rows * columns, outputs), jnp.float32)
    for frame_tap in range(3):
        for row_tap in range(3):
            window = padded[:, frame_tap:frame_tap + frames, row_tap:row_tap + rows]
            stacked = jnp.concatenate([window[:, :, :, col_tap:col_tap + columns] for col_tap in range(3)], axis=-1)
            kernel = weight[frame_tap, row_tap].reshape(3 * channels, outputs)
            summed = summed + jnp.dot(stacked.reshape(-1, 3 * channels), kernel, preferred_element_type=jnp.float32)
    return summed.reshape(count, frames, rows, columns, outputs)

def earlier_frames(slot_cache, slots, keep_mask):
    chosen = jnp.take(slot_cache, slots, axis=0)
    return jnp.where(keep_mask[:, None, None, None, None], chosen, jnp.zeros_like(chosen))

def to_space(values):
    count, frames, rows, columns, channels = values.shape
    quarter = channels // 4
    spread = values.reshape(count, frames, rows, columns, 2, 2, quarter)
    spread = spread.transpose(0, 1, 2, 4, 3, 5, 6)
    return spread.reshape(count, frames, 2 * rows, 2 * columns, quarter)

def reference(latents, cache_first, cache_second, gain_first, gain_second, w_first, w_second, cache_slot, block_index):
    keep_mask = block_index > 0
    first_act = norm_silu(latents.astype(jnp.float32), gain_first).astype(jnp.bfloat16)
    frames = jnp.concatenate([earlier_frames(cache_first, cache_slot, keep_mask), first_act], axis=1)
    frames = jnp.pad(frames, ((0, 0), (0, 0), (1, 1), (0, 0), (0, 0)))
    first_conv = causal_conv(frames, w_first).astype(jnp.bfloat16)
    upsampled = to_space(first_conv)
    second_act = norm_silu(upsampled.astype(jnp.float32), gain_second).astype(jnp.bfloat16)
    second = jnp.concatenate([earlier_frames(cache_second, cache_slot, keep_mask), second_act], axis=1)
    second = jnp.pad(second, ((0, 0), (0, 0), (1, 1), (0, 0), (0, 0)))
    branch = causal_conv(second, w_second).astype(jnp.bfloat16)
    return (upsampled.astype(jnp.float32) + branch.astype(jnp.float32)).astype(jnp.bfloat16)
```

```python
import jax
import jax.numpy as jnp
from jax import lax
from jax.experimental import pallas as pl
from jax.experimental.pallas import tpu as pltpu
from jax.sharding import PartitionSpec as P

epsilon = 1e-06
MESH = pl.DeviceIdType.MESH
F32 = jnp.float32
BF16 = jnp.bfloat16


def norm_silu(values, gain):
    mean_square = jnp.mean(values * values, axis=-1, keepdims=True)
    return jax.nn.silu(values * lax.rsqrt(mean_square + epsilon) * gain)


def dot_nk(left, right):
    return lax.dot_general(left, right, (((1,), (1,)), ((), ())), preferred_element_type=F32)


def kernel(
    slot_hbm, block_hbm, gain1_hbm, gain2_hbm, lat, c1, c2, w1, w2,
    out_ref, base_ref,
    LT, A1, A2, KA, KO, KZ, W11, W02, W2, C, ES, ER, S, U, H, RB, Q,
    loc, s1, r1, s2, r2, sc, rc, se, re, su, ru, sw, rw, sq, rq,
    slot_ref, block_ref, gain1_ref, gain2_ref, gsem,
):
    K = (KA, KO, KZ)
    p = lax.axis_index("strm")
    h = lax.axis_index("band")
    bands = lax.axis_size("band")
    core = lax.rem(p, 2)
    half = p // 2
    mate = p + 1 - 2 * core
    over = lax.rem(p + 2, 4)
    cross = lax.rem(mate + 2, 4)
    not_top = h > 0
    not_bottom = h < bands - 1

    def load(src, dst, i):
        copy = pltpu.make_async_copy(src, dst, loc.at[i])
        copy.start()
        return copy

    lat_copy = load(lat, LT, 0)
    smalls = [
        pltpu.make_async_copy(src, dst, gsem.at[i])
        for i, (src, dst) in enumerate(
            (
                (gain1_hbm, gain1_ref),
                (gain2_hbm, gain2_ref),
                (slot_hbm, slot_ref),
                (block_hbm, block_ref),
            )
        )
    ]
    for copy in smalls:
        copy.start()
    c1_copy = load(c1, KO.at[p], 1)
    c2_copy = load(c2, C.at[p], 2)

    barrier = pltpu.get_barrier_semaphore()
    for other in (mate, over, cross):
        pl.semaphore_signal(barrier, inc=1, device_id={"strm": other}, device_id_type=MESH)

    def greet(band):
        for other in (p, mate):
            pl.semaphore_signal(
                barrier, inc=1, device_id={"strm": other, "band": band}, device_id_type=MESH
            )

    pl.when(not_top)(lambda: greet(h - 1))
    pl.when(not_bottom)(lambda: greet(h + 1))
    w1_mid = load(w1.at[:, 1], W11, 3)
    w2_copy = load(w2, W2.at[:, pl.ds(pl.multiple_of(48 * core, 16), 48)], 6)
    w1_top = load(w1.at[:, 0], W02.at[:, :, :, pl.ds(0, 384)], 4)
    w1_bot = load(w1.at[:, 2], W02.at[:, :, :, pl.ds(384, 384)], 5)

    @pl.when(h == 0)
    def _():
        KA[...] = jnp.zeros((4, 32, 384), BF16)
        A2[2:4, :, 0:384] = jnp.zeros((2, 64, 384), BF16)
        ER[0] = jnp.zeros((2, 2, 32, 192), BF16)
        U[0] = jnp.zeros((2, 2, 2, 16, 192), BF16)

    @pl.when(h == bands - 1)
    def _():
        KZ[...] = jnp.zeros((4, 32, 384), BF16)
        A2[2:4, :, 384:768] = jnp.zeros((2, 64, 384), BF16)
        ER[1] = jnp.zeros((2, 2, 32, 192), BF16)
        U[3] = jnp.zeros((2, 2, 2, 16, 192), BF16)

    def cells(s):
        return pl.ds(pl.multiple_of(16 * s, 16), 16)

    def acts(j, s):
        if j == 1:
            return A1.at[2:4, cells(s)]
        return A2.at[2:4, cells(s), pl.ds(192 * j, 384)]

    for copy in smalls:
        copy.wait()
    gain1 = gain1_ref[...].reshape(1, 384)
    gain2 = gain2_ref[...].reshape(1, 192)
    lat_copy.wait()
    first_act = norm_silu(LT[...].astype(F32), gain1).astype(BF16)
    A1[2, cells(p)] = first_act[0:16]
    A1[3, cells(p)] = first_act[16:32]
    c1_copy.wait()

    peers = 3 + 2 * not_top.astype(jnp.int32) + 2 * not_bottom.astype(jnp.int32)
    pl.semaphore_wait(barrier, peers)

    def remote(src, dst, send, recv, strm, band):
        return pltpu.make_async_remote_copy(
            src_ref=src, dst_ref=dst, send_sem=send, recv_sem=recv,
            device_id={"strm": strm, "band": band}, device_id_type=MESH,
        )

    class Row:
        def __init__(self, i, j_src, j_dst, s, strm, band):
            self.parts = (
                remote(K[j_src].at[s], K[j_dst].at[s], s2.at[i], r2.at[j_dst, s], strm, band),
                remote(acts(j_src, s), acts(j_dst, s), s1.at[i], r1.at[j_dst, s], strm, band),
            )

        def start(self):
            for part in self.parts:
                part.start()

        def wait_send(self):
            for part in self.parts:
                part.wait_send()

    def arrive(j, s):
        for part in Row(0, j, j, s, mate, h).parts:
            part.wait_recv()

    near = [Row(i, 1, 1, p, d, h) for i, d in enumerate((over, cross, mate))]
    above = [Row(3 + i, 1, 2, p, d, h - 1) for i, d in enumerate((p, mate))]
    below = [Row(5 + i, 1, 0, p, d, h + 1) for i, d in enumerate((p, mate))]
    above2 = [Row(7 + i, 1, 2, over, d, h - 1) for i, d in enumerate((p, mate))]
    below2 = [Row(9 + i, 1, 0, over, d, h + 1) for i, d in enumerate((p, mate))]

    def go(rows):
        for row in rows:
            row.start()

    go(near[:2])
    pl.when(not_top)(lambda: go(above))
    pl.when(not_bottom)(lambda: go(below))
    go(near[2:])
    c2_copy.wait()
    c_over = remote(C.at[p], C.at[p], sc.at[0], rc.at[p], over, h)
    c_mate = remote(C.at[p], C.at[p], sc.at[1], rc.at[p], mate, h)
    c_over.start()
    c_mate.start()

    arrive(1, over)
    pl.when(not_top)(lambda: go(above2))
    pl.when(not_bottom)(lambda: go(below2))
    def carrive(s):
        remote(C.at[s], C.at[s], sc.at[0], rc.at[s], mate, h).wait_recv()

    carrive(over)
    c_fwd = remote(C.at[over], C.at[over], sc.at[2], rc.at[over], mate, h)
    c_fwd.start()

    arrive(1, mate)
    arrive(1, cross)

    def fill(j):
        for s in range(4):
            piece = K[j][slot_ref[s]].astype(F32)
            piece = jnp.where(block_ref[s] > 0, piece, jnp.zeros_like(piece)).astype(BF16)
            for f in range(2):
                block = piece[16 * f : 16 * f + 16]
                if j == 1:
                    A1[f, 16 * s : 16 * s + 16] = block
                else:
                    A2[f, 16 * s : 16 * s + 16, 192 * j : 192 * j + 384] = block

    fill(1)
    w1_mid.wait()
    total = [None] * 3

    def taps(stack, weight, depth):
        for i in range(3):
            rows = stack[i : i + 2].reshape(128, depth)
            for l in range(3):
                term = dot_nk(rows, weight[i, l])
                total[l] = term if total[l] is None else total[l] + term

    taps(A1, W11, 384)
    w2_copy.wait()

    def w2_rows(c):
        return W2.at[:, pl.ds(pl.multiple_of(48 * c, 16), 48)]

    w_mate = remote(w2_rows(core), w2_rows(core), sw, rw, mate, h)
    w_mate.start()

    carrive(mate)
    carrive(cross)
    rows32 = lax.broadcasted_iota(jnp.int32, (32, 32), 0)
    cols32 = lax.broadcasted_iota(jnp.int32, (32, 32), 1)
    split = jnp.where(cols32 == 2 * lax.rem(rows32, 16) + rows32 // 16, 1.0, 0.0).astype(BF16)
    weave = jnp.where(rows32 == 2 * lax.rem(cols32, 16) + cols32 // 16, 1.0, 0.0).astype(BF16)

    def place(block, frame, row, sp):
        moved = jnp.dot(split, block, preferred_element_type=F32).astype(BF16)
        H[frame, row, sp * 32 : sp * 32 + 32] = moved
        return moved

    for sp in range(2):
        s = core + 2 * sp
        chosen = C[slot_ref[s]]
        chosen = jnp.where(block_ref[s] > 0, chosen.astype(F32), 0.0).astype(BF16)
        for f in range(2):
            for row in range(2):
                ES[row, sp, f] = place(chosen[f, row], f, row + 1, sp)
    e_up = remote(ES.at[0], ER.at[1], se.at[0], re.at[1], p, h - 1)
    e_down = remote(ES.at[1], ER.at[0], se.at[1], re.at[0], p, h + 1)
    pl.when(not_top)(e_up.start)
    pl.when(not_bottom)(e_down.start)

    @pl.when(not_top)
    def _():
        for s in (p, mate, over, cross):
            arrive(0, s)

    @pl.when(not_bottom)
    def _():
        for s in (p, mate, over, cross):
            arrive(2, s)

    fill(0)
    fill(2)
    w1_top.wait()
    w1_bot.wait()
    taps(A2, W02, 768)
    column = lax.rem(lax.broadcasted_iota(jnp.int32, (128, 192), 0), 16)
    up = (
        total[1]
        + jnp.where(column == 0, 0.0, pltpu.roll(total[0], 1, 0))
        + jnp.where(column == 15, 0.0, pltpu.roll(total[2], 127, 0))
    ).astype(BF16)
    for k in range(2):
        for sp in range(2):
            for t in range(2):
                start = (t * 4 + k + 2 * sp) * 16
                S[k, sp, t] = up[start : start + 16]

    def ucopy(i, d, row, band):
        return remote(
            S.at[lax.rem(d, 2)], U.at[row, :, :, core], su.at[i], ru.at[row, half, core], d, band
        )

    u_own = [ucopy(i, d, 1 + half, h) for i, d in enumerate((over, cross, mate))]
    u_up = [ucopy(3 + i, d, 3, h - 1) for i, d in enumerate((cross, over, p, mate))]
    u_down = [ucopy(3 + i, d, 0, h + 1) for i, d in enumerate((cross, over, p, mate))]
    sends_up = jnp.logical_and(half == 0, not_top)
    sends_down = jnp.logical_and(half == 1, not_bottom)
    u_own[0].start()
    u_own[1].start()

    @pl.when(sends_up)
    def _():
        for copy in u_up:
            copy.start()

    @pl.when(sends_down)
    def _():
        for copy in u_down:
            copy.start()

    u_own[2].start()
    U[1 + half, :, :, core] = S[core]

    def wait_edge(n):
        remote(ES.at[0], ER.at[n], se.at[0], re.at[n], mate, h).wait_recv()

    pl.when(not_top)(lambda: wait_edge(0))
    pl.when(not_bottom)(lambda: wait_edge(1))
    for sp in range(2):
        for f in range(2):
            H[f, 0, sp * 32 : sp * 32 + 32] = ER[0, sp, f]
            H[f, 3, sp * 32 : sp * 32 + 32] = ER[1, sp, f]
    remote(w2_rows(1 - core), w2_rows(1 - core), sw, rw, mate, h).wait_recv()
    partial = [None]

    def tap(i, j):
        at = i * 9 + j * 3
        term = dot_nk(
            H[i : i + 2, j : j + 2].reshape(256, 192), W2[at : at + 3].reshape(288, 192)
        )
        partial[0] = term if partial[0] is None else partial[0] + term

    for j in range(3):
        tap(0, j)

    def uarrive(row, b, a):
        remote(S.at[0], U.at[row, :, :, b], su.at[0], ru.at[row, a, b], mate, h).wait_recv()

    for b in range(2):
        for a in range(2):

            @pl.when(p != 2 * a + b)
            def _():
                uarrive(1 + a, b, a)

    def advance(row):
        x = U[row].reshape(128, 192).astype(F32)
        act = norm_silu(x, gain2).astype(BF16)
        for sp in range(2):
            for t in range(2):
                start = (sp * 2 + t) * 32
                H[2 + t, row, sp * 32 : sp * 32 + 32] = act[start : start + 32]

    advance(1)
    advance(2)
    tap(1, 1)
    tap(2, 1)

    @pl.when(not_top)
    def _():
        uarrive(0, 0, 1)
        uarrive(0, 1, 1)

    @pl.when(not_bottom)
    def _():
        uarrive(3, 0, 0)
        uarrive(3, 1, 0)

    advance(0)
    advance(3)
    for j in (0, 2):
        for i in (1, 2):
            tap(i, j)
    full = partial[0]
    y0, y1, y2 = full[:, 0:96], full[:, 96:192], full[:, 192:288]
    rows = lax.broadcasted_iota(jnp.int32, (256, 96), 0)
    even = lax.rem(rows // 16, 2) == 0
    place_w = lax.rem(rows, 16)
    before = jnp.where(
        even, jnp.where(place_w == 0, 0.0, pltpu.roll(y0, 241, 0)), pltpu.roll(y0, 16, 0)
    )
    after = jnp.where(
        even, pltpu.roll(y2, 240, 0), jnp.where(place_w == 15, 0.0, pltpu.roll(y2, 15, 0))
    )
    result = (y1 + before + after).astype(BF16)
    for ta in range(4):
        for sp in range(2):
            start = ta * 64 + sp * 32
            RB[sp, ta] = result[start : start + 32]
    q = remote(RB.at[1 - half], Q, sq, rq, over, h)
    q.start()
    for t in range(2):
        for a in range(2):
            block = U[1 + a, half, t].reshape(32, 192)
            base_ref[t, a] = jnp.dot(weave, block, preferred_element_type=F32).astype(BF16)
    mine = RB[half].astype(F32)
    q.wait_recv()
    theirs = Q[...].astype(F32)
    low = jnp.where(half == 0, mine, theirs)
    high = jnp.where(half == 0, theirs, mine)
    branch = jnp.concatenate([low, high], axis=-1).astype(BF16)
    for t in range(2):
        for a in range(2):
            woven = jnp.dot(weave, branch[t * 2 + a], preferred_element_type=F32)
            out_ref[t, a] = (base_ref[t, a].astype(F32) + woven.astype(BF16).astype(F32)).astype(BF16)

    q.wait_send()
    for copy in (*near, c_over, c_mate, c_fwd, w_mate, *u_own):
        copy.wait_send()

    def left(rows):
        for row in rows:
            row.wait_send()

    pl.when(not_top)(lambda: left(above + above2 + [e_up]))
    pl.when(not_bottom)(lambda: left(below + below2 + [e_down]))

    @pl.when(sends_up)
    def _():
        for copy in u_up:
            copy.wait_send()

    @pl.when(sends_down)
    def _():
        for copy in u_down:
            copy.wait_send()


def hbm(x):
    return pltpu.with_memory_space_constraint(x, pltpu.HBM)


def body(
    latents, cache_first, cache_second, gain_first, gain_second, w_first, w_second,
    cache_slot, block_index,
):
    any_spec = pl.BlockSpec(memory_space=pltpu.HBM)
    vmem = pl.BlockSpec(memory_space=pltpu.VMEM)
    smem = pl.BlockSpec(memory_space=pltpu.SMEM)
    dma = pltpu.SemaphoreType.DMA
    decoded = pl.pallas_call(
        kernel,
        out_shape=jax.ShapeDtypeStruct((2, 2, 32, 192), BF16),
        in_specs=[any_spec] * 9,
        out_specs=vmem,
        scratch_shapes=[
            pltpu.VMEM((2, 2, 32, 192), BF16),
            pltpu.VMEM((32, 384), BF16),
            pltpu.VMEM((4, 64, 384), BF16),
            pltpu.VMEM((4, 64, 768), BF16),
            pltpu.VMEM((4, 32, 384), BF16),
            pltpu.VMEM((4, 32, 384), BF16),
            pltpu.VMEM((4, 32, 384), BF16),
            pltpu.VMEM((3, 3, 192, 384), BF16),
            pltpu.VMEM((3, 3, 192, 768), BF16),
            pltpu.VMEM((27, 96, 192), BF16),
            pltpu.VMEM((4, 2, 2, 32, 192), BF16),
            pltpu.VMEM((2, 2, 2, 32, 192), BF16),
            pltpu.VMEM((2, 2, 2, 32, 192), BF16),
            pltpu.VMEM((2, 2, 2, 16, 192), BF16),
            pltpu.VMEM((4, 2, 2, 2, 16, 192), BF16),
            pltpu.VMEM((4, 4, 64, 192), BF16),
            pltpu.VMEM((2, 4, 32, 96), BF16),
            pltpu.VMEM((4, 32, 96), BF16),
            dma((7,)),
            dma((11,)),
            dma((3, 4)),
            dma((11,)),
            dma((3, 4)),
            dma((3,)),
            dma((4,)),
            dma((2,)),
            dma((2,)),
            dma((7,)),
            dma((4, 2, 2)),
            dma,
            dma,
            dma,
            dma,
            pltpu.SMEM((4,), jnp.int32),
            pltpu.SMEM((4,), jnp.int32),
            pltpu.VMEM((384,), F32),
            pltpu.VMEM((192,), F32),
            dma((4,)),
        ],
        compiler_params=pltpu.CompilerParams(
            collective_id=0, has_side_effects=True, vmem_limit_bytes=40 * 1024 * 1024
        ),
    )(
        hbm(cache_slot),
        hbm(block_index),
        hbm(gain_first),
        hbm(gain_second),
        hbm(latents.reshape(32, 384)),
        hbm(cache_first.reshape(32, 384)),
        hbm(cache_second.reshape(2, 2, 32, 192)),
        hbm(w_first.transpose(0, 1, 2, 4, 3)),
        hbm(w_second.transpose(0, 1, 2, 4, 3).reshape(27, 48, 192)),
    )
    return decoded.reshape(1, 2, 2, 32, 192)


def solution(mesh):
    in_specs = (
        P(("grp", "strm"), None, "band", None, None),
        P(("grp", "strm"), None, "band", None, None),
        P(("grp", "strm"), None, "band", None, None),
        P(),
        P(),
        P(None, None, None, None, "strm"),
        P(None, None, None, None, "strm"),
        P("grp"),
        P("grp"),
    )
    out_specs = P(("grp", "strm"), None, "band", None, None)
    return jax.shard_map(body, mesh=mesh, in_specs=in_specs, out_specs=out_specs, check_vma=False)
```

```python
import jax
import jax.numpy as jnp
from jax import lax
from jax.experimental import pallas as pl
from jax.experimental.pallas import tpu as pltpu
from jax.sharding import PartitionSpec as P

epsilon = 1e-06
MESH = pl.DeviceIdType.MESH
F32 = jnp.float32
BF16 = jnp.bfloat16


def norm_silu(values, gain):
    mean_square = jnp.mean(values * values, axis=-1, keepdims=True)
    return jax.nn.silu(values * lax.rsqrt(mean_square + epsilon) * gain)


def dot_nk(left, right):
    return lax.dot_general(left, right, (((1,), (1,)), ((), ())), preferred_element_type=F32)


def kernel(
    slot_hbm, block_hbm, gain1_hbm, gain2_hbm, lat, c1, c2, w1, w2,
    out_ref, base_ref,
    LT, A1, A2, KA, KO, KZ, W11, W02, W2, C, EB, XR, S, U, H, RB, Q,
    loc, s1, r1, s2, r2, sc, rc, se, re, su, ru, sw, rw, sq, rq,
    slot_ref, block_ref, gain1_ref, gain2_ref, gsem,
):
    K = (KA, KO, KZ)
    p = lax.axis_index("strm")
    h = lax.axis_index("band")
    bands = lax.axis_size("band")
    core = lax.rem(p, 2)
    half = p // 2
    mate = p + 1 - 2 * core
    over = lax.rem(p + 2, 4)
    cross = lax.rem(mate + 2, 4)
    not_top = h > 0
    not_bottom = h < bands - 1

    def load(src, dst, i):
        copy = pltpu.make_async_copy(src, dst, loc.at[i])
        copy.start()
        return copy

    lat_copy = load(lat, LT, 0)
    smalls = [
        pltpu.make_async_copy(src, dst, gsem.at[i])
        for i, (src, dst) in enumerate(
            (
                (gain1_hbm, gain1_ref),
                (gain2_hbm, gain2_ref),
                (slot_hbm, slot_ref),
                (block_hbm, block_ref),
            )
        )
    ]
    for copy in smalls:
        copy.start()
    c1_copy = load(c1, KO.at[p], 1)
    c2_copy = load(c2, C.at[p], 2)

    barrier = pltpu.get_barrier_semaphore()
    for other in (mate, over, cross):
        pl.semaphore_signal(barrier, inc=1, device_id={"strm": other}, device_id_type=MESH)

    def greet(band):
        for other in (p, mate):
            pl.semaphore_signal(
                barrier, inc=1, device_id={"strm": other, "band": band}, device_id_type=MESH
            )

    pl.when(not_top)(lambda: greet(h - 1))
    pl.when(not_bottom)(lambda: greet(h + 1))
    w1_mid = load(w1.at[:, 1], W11, 3)
    w2_copy = load(w2, W2.at[:, pl.ds(pl.multiple_of(48 * core, 16), 48)], 6)
    w1_top = load(w1.at[:, 0], W02.at[:, :, :, pl.ds(0, 384)], 4)
    w1_bot = load(w1.at[:, 2], W02.at[:, :, :, pl.ds(384, 384)], 5)

    W2[:, 96:128] = jnp.zeros((27, 32, 192), BF16)

    @pl.when(h == 0)
    def _():
        KA[...] = jnp.zeros((4, 32, 384), BF16)
        A2[2:4, :, 0:384] = jnp.zeros((2, 64, 384), BF16)
        XR[0] = jnp.zeros((2, 2, 32, 128), BF16)

    @pl.when(h == bands - 1)
    def _():
        KZ[...] = jnp.zeros((4, 32, 384), BF16)
        A2[2:4, :, 384:768] = jnp.zeros((2, 64, 384), BF16)
        XR[1] = jnp.zeros((2, 2, 32, 128), BF16)

    def cells(s):
        return pl.ds(pl.multiple_of(16 * s, 16), 16)

    def acts(j, s):
        if j == 1:
            return A1.at[2:4, cells(s)]
        return A2.at[2:4, cells(s), pl.ds(192 * j, 384)]

    for copy in smalls:
        copy.wait()
    gain1 = gain1_ref[...].reshape(1, 384)
    gain2 = gain2_ref[...].reshape(1, 192)
    lat_copy.wait()
    first_act = norm_silu(LT[...].astype(F32), gain1).astype(BF16)
    A1[2, cells(p)] = first_act[0:16]
    A1[3, cells(p)] = first_act[16:32]
    c1_copy.wait()

    peers = 3 + 2 * not_top.astype(jnp.int32) + 2 * not_bottom.astype(jnp.int32)
    pl.semaphore_wait(barrier, peers)

    def remote(src, dst, send, recv, strm, band):
        return pltpu.make_async_remote_copy(
            src_ref=src, dst_ref=dst, send_sem=send, recv_sem=recv,
            device_id={"strm": strm, "band": band}, device_id_type=MESH,
        )

    class Row:
        def __init__(self, i, j_src, j_dst, s, strm, band):
            self.parts = (
                remote(K[j_src].at[s], K[j_dst].at[s], s2.at[i], r2.at[j_dst, s], strm, band),
                remote(acts(j_src, s), acts(j_dst, s), s1.at[i], r1.at[j_dst, s], strm, band),
            )

        def start(self):
            for part in self.parts:
                part.start()

        def wait_send(self):
            for part in self.parts:
                part.wait_send()

    def arrive(j, s):
        for part in Row(0, j, j, s, mate, h).parts:
            part.wait_recv()

    near = [Row(i, 1, 1, p, d, h) for i, d in enumerate((over, cross, mate))]
    above = [Row(3 + i, 1, 2, p, d, h - 1) for i, d in enumerate((p, mate))]
    below = [Row(5 + i, 1, 0, p, d, h + 1) for i, d in enumerate((p, mate))]
    above2 = [Row(7 + i, 1, 2, over, d, h - 1) for i, d in enumerate((p, mate))]
    below2 = [Row(9 + i, 1, 0, over, d, h + 1) for i, d in enumerate((p, mate))]

    def go(rows):
        for row in rows:
            row.start()

    go(near[:2])
    pl.when(not_top)(lambda: go(above))
    pl.when(not_bottom)(lambda: go(below))
    go(near[2:])
    c2_copy.wait()
    c_over = remote(C.at[p], C.at[p], sc.at[0], rc.at[p], over, h)
    c_mate = remote(C.at[p], C.at[p], sc.at[1], rc.at[p], mate, h)
    c_over.start()
    c_mate.start()

    arrive(1, over)
    pl.when(not_top)(lambda: go(above2))
    pl.when(not_bottom)(lambda: go(below2))
    def carrive(s):
        remote(C.at[s], C.at[s], sc.at[0], rc.at[s], mate, h).wait_recv()

    carrive(over)
    c_fwd = remote(C.at[over], C.at[over], sc.at[2], rc.at[over], mate, h)
    c_fwd.start()

    arrive(1, mate)
    arrive(1, cross)

    def fill(j):
        for s in range(4):
            piece = K[j][slot_ref[s]].astype(F32)
            piece = jnp.where(block_ref[s] > 0, piece, jnp.zeros_like(piece)).astype(BF16)
            for f in range(2):
                block = piece[16 * f : 16 * f + 16]
                if j == 1:
                    A1[f, 16 * s : 16 * s + 16] = block
                else:
                    A2[f, 16 * s : 16 * s + 16, 192 * j : 192 * j + 384] = block

    fill(1)
    w1_mid.wait()
    total = [None] * 3

    def taps(stack, weight, depth):
        for i in range(3):
            rows = stack[i : i + 2].reshape(128, depth)
            for l in range(3):
                term = dot_nk(rows, weight[i, l])
                total[l] = term if total[l] is None else total[l] + term

    taps(A1, W11, 384)
    w2_copy.wait()

    def w2_rows(c):
        return W2.at[:, pl.ds(pl.multiple_of(48 * c, 16), 48)]

    w_mate = remote(w2_rows(core), w2_rows(core), sw, rw, mate, h)
    w_mate.start()

    carrive(mate)
    carrive(cross)
    rows32 = lax.broadcasted_iota(jnp.int32, (32, 32), 0)
    cols32 = lax.broadcasted_iota(jnp.int32, (32, 32), 1)
    split = jnp.where(cols32 == 2 * lax.rem(rows32, 16) + rows32 // 16, 1.0, 0.0).astype(BF16)
    weave = jnp.where(rows32 == 2 * lax.rem(cols32, 16) + cols32 // 16, 1.0, 0.0).astype(BF16)

    def place(block, frame, row, sp):
        moved = jnp.dot(split, block, preferred_element_type=F32).astype(BF16)
        H[frame, row, sp * 32 : sp * 32 + 32] = moved

    for sp in range(2):
        s = core + 2 * sp
        chosen = C[slot_ref[s]]
        chosen = jnp.where(block_ref[s] > 0, chosen.astype(F32), 0.0).astype(BF16)
        for f in range(2):
            for row in range(2):
                place(chosen[f, row], f, row, sp)

    @pl.when(not_top)
    def _():
        for s in (p, mate, over, cross):
            arrive(0, s)

    @pl.when(not_bottom)
    def _():
        for s in (p, mate, over, cross):
            arrive(2, s)

    fill(0)
    fill(2)
    w1_top.wait()
    w1_bot.wait()
    taps(A2, W02, 768)
    column = lax.rem(lax.broadcasted_iota(jnp.int32, (128, 192), 0), 16)
    up = (
        total[1]
        + jnp.where(column == 0, 0.0, pltpu.roll(total[0], 1, 0))
        + jnp.where(column == 15, 0.0, pltpu.roll(total[2], 127, 0))
    ).astype(BF16)
    for k in range(2):
        for t in range(2):
            lo, hi = (up[(t * 4 + k + n) * 16 : (t * 4 + k + n) * 16 + 16] for n in (0, 2))
            S[k, t, :, 0:128] = lo[:, 0:128]
            S[k, t, :, 128:256] = hi[:, 0:128]
            S[k, t, :, 256:384] = jnp.concatenate([lo[:, 128:192], hi[:, 128:192]], axis=-1)

    def ucopy(i, d):
        return remote(
            S.at[lax.rem(d, 2)], U.at[half, :, core], su.at[i], ru.at[half, core], d, h
        )

    u_own = [ucopy(i, d) for i, d in enumerate((over, cross, mate))]
    for copy in u_own:
        copy.start()
    U[half, :, core] = S[core]
    remote(w2_rows(1 - core), w2_rows(1 - core), sw, rw, mate, h).wait_recv()
    def taps2(i, j, frames):
        n = len(frames)
        at = i * 9 + j * 3
        term = dot_nk(
            H[frames[0] : frames[0] + n].reshape(n * 128, 192), W2[at : at + 3].reshape(384, 192)
        )
        return term

    first = [[None] * 3 for _ in range(2)]
    for j in range(3):
        both = taps2(0, j, (0, 1))
        first[0][j] = both[0:128] + taps2(1, j, (1,))
        first[1][j] = both[128:256]

    def uarrive(b, a):
        remote(S.at[0], U.at[a, :, b], su.at[0], ru.at[a, b], mate, h).wait_recv()

    for b in range(2):
        for a in range(2):

            @pl.when(p != 2 * a + b)
            def _():
                uarrive(b, a)

    def advance(row):
        x = U[row].reshape(64, 384).astype(F32)
        parts = (
            jnp.concatenate([x[:, 0:128], x[:, 256:320]], axis=-1),
            jnp.concatenate([x[:, 128:256], x[:, 320:384]], axis=-1),
        )
        own = jnp.where(half == 0, parts[0], parts[1])
        for t in range(2):
            base_ref[t, row] = own[32 * t : 32 * t + 32]
        for sp in range(2):
            act = norm_silu(parts[sp], gain2).astype(BF16)
            for t in range(2):
                H[2 + t, row, sp * 32 : sp * 32 + 32] = act[32 * t : 32 * t + 32]

    advance(0)
    advance(1)

    def total2(j):
        both = taps2(2, j, (2, 3))
        return (first[0][j] + both[0:128], first[1][j] + both[128:256] + taps2(1, j, (2,)))

    def weave_columns(full):
        count = full.shape[0]
        y0, y1, y2 = full[:, 0:128], full[:, 128:256], full[:, 256:384]
        rows = lax.broadcasted_iota(jnp.int32, (count, 128), 0)
        even = lax.rem(rows // 16, 2) == 0
        place_w = lax.rem(rows, 16)
        before = jnp.where(
            even,
            jnp.where(place_w == 0, 0.0, pltpu.roll(y0, count - 15, 0)),
            pltpu.roll(y0, 16, 0),
        )
        after = jnp.where(
            even,
            pltpu.roll(y2, count - 16, 0),
            jnp.where(place_w == 15, 0.0, pltpu.roll(y2, 15, 0)),
        )
        return y1 + before + after

    def edge(n, totals):
        for t in range(2):
            result = weave_columns(totals[t][64 * n : 64 * n + 64]).astype(BF16)
            for sp in range(2):
                EB[n, sp, t] = result[32 * sp : 32 * sp + 32]

    def ecopies(n, band):
        return [
            remote(EB.at[n, sp], XR.at[1 - n, half], se.at[n, i], re.at[1 - n, half], d, band)
            for i, (sp, d) in enumerate(((1 - half, over), (half, p)))
        ]

    e_up = ecopies(0, h - 1)
    e_down = ecopies(1, h + 1)

    def launch(copies):
        for copy in copies:
            copy.start()

    low_taps = total2(2)
    edge(0, low_taps)
    pl.when(not_top)(lambda: launch(e_up))
    high_taps = total2(0)
    edge(1, high_taps)
    pl.when(not_bottom)(lambda: launch(e_down))
    mid_taps = total2(1)
    mine = [[None] * 2 for _ in range(2)]
    for t in range(2):
        for a in range(2):
            other = low_taps[t][64:128] if a == 0 else high_taps[t][0:64]
            result = weave_columns(mid_taps[t][64 * a : 64 * a + 64] + other)
            for sp in range(2):
                RB[sp, t * 2 + a] = result[32 * sp : 32 * sp + 32].astype(BF16)
            mine[t][a] = jnp.where(half == 0, result[0:32], result[32:64])
    q = remote(RB.at[1 - half], Q, sq, rq, over, h)
    q.start()

    def earrive(n):
        for g in range(2):
            remote(EB.at[0, 0], XR.at[n, g], se.at[0, 0], re.at[n, g], over, h).wait_recv()

    pl.when(not_top)(lambda: earrive(0))
    pl.when(not_bottom)(lambda: earrive(1))
    q.wait_recv()
    for t in range(2):
        for a in range(2):
            theirs = Q[t * 2 + a].astype(F32)
            low = jnp.where(half == 0, mine[t][a], theirs) + XR[a, 0, t].astype(F32)
            high = jnp.where(half == 0, theirs, mine[t][a]) + XR[a, 1, t].astype(F32)
            branch = jnp.concatenate([low[:, 0:96], high[:, 0:96]], axis=-1).astype(BF16)
            total_ta = (base_ref[t, a] + branch.astype(F32)).astype(BF16)
            out_ref[t, a] = jnp.dot(weave, total_ta, preferred_element_type=F32).astype(BF16)

    q.wait_send()
    for copy in (*near, c_over, c_mate, c_fwd, w_mate, *u_own):
        copy.wait_send()

    def left(rows):
        for row in rows:
            row.wait_send()

    pl.when(not_top)(lambda: left(above + above2 + e_up))
    pl.when(not_bottom)(lambda: left(below + below2 + e_down))


def hbm(x):
    return pltpu.with_memory_space_constraint(x, pltpu.HBM)


def body(
    latents, cache_first, cache_second, gain_first, gain_second, w_first, w_second,
    cache_slot, block_index,
):
    any_spec = pl.BlockSpec(memory_space=pltpu.HBM)
    vmem = pl.BlockSpec(memory_space=pltpu.VMEM)
    smem = pl.BlockSpec(memory_space=pltpu.SMEM)
    dma = pltpu.SemaphoreType.DMA
    decoded = pl.pallas_call(
        kernel,
        out_shape=jax.ShapeDtypeStruct((2, 2, 32, 192), BF16),
        in_specs=[any_spec] * 9,
        out_specs=vmem,
        scratch_shapes=[
            pltpu.VMEM((2, 2, 32, 192), F32),
            pltpu.VMEM((32, 384), BF16),
            pltpu.VMEM((4, 64, 384), BF16),
            pltpu.VMEM((4, 64, 768), BF16),
            pltpu.VMEM((4, 32, 384), BF16),
            pltpu.VMEM((4, 32, 384), BF16),
            pltpu.VMEM((4, 32, 384), BF16),
            pltpu.VMEM((3, 3, 192, 384), BF16),
            pltpu.VMEM((3, 3, 192, 768), BF16),
            pltpu.VMEM((27, 128, 192), BF16),
            pltpu.VMEM((4, 2, 2, 32, 192), BF16),
            pltpu.VMEM((2, 2, 2, 32, 128), BF16),
            pltpu.VMEM((2, 2, 2, 32, 128), BF16),
            pltpu.VMEM((2, 2, 16, 384), BF16),
            pltpu.VMEM((2, 2, 2, 16, 384), BF16),
            pltpu.VMEM((4, 2, 64, 192), BF16),
            pltpu.VMEM((2, 4, 32, 128), BF16),
            pltpu.VMEM((4, 32, 128), BF16),
            dma((7,)),
            dma((11,)),
            dma((3, 4)),
            dma((11,)),
            dma((3, 4)),
            dma((3,)),
            dma((4,)),
            dma((2, 2)),
            dma((2, 2)),
            dma((3,)),
            dma((2, 2)),
            dma,
            dma,
            dma,
            dma,
            pltpu.SMEM((4,), jnp.int32),
            pltpu.SMEM((4,), jnp.int32),
            pltpu.VMEM((384,), F32),
            pltpu.VMEM((192,), F32),
            dma((4,)),
        ],
        compiler_params=pltpu.CompilerParams(
            collective_id=0, has_side_effects=True, vmem_limit_bytes=40 * 1024 * 1024
        ),
    )(
        hbm(cache_slot),
        hbm(block_index),
        hbm(gain_first),
        hbm(gain_second),
        hbm(latents.reshape(32, 384)),
        hbm(cache_first.reshape(32, 384)),
        hbm(cache_second.reshape(2, 2, 32, 192)),
        hbm(w_first.transpose(0, 1, 2, 4, 3)),
        hbm(w_second.transpose(0, 1, 2, 4, 3).reshape(27, 48, 192)),
    )
    return decoded.reshape(1, 2, 2, 32, 192)


def solution(mesh):
    in_specs = (
        P(("grp", "strm"), None, "band", None, None),
        P(("grp", "strm"), None, "band", None, None),
        P(("grp", "strm"), None, "band", None, None),
        P(),
        P(),
        P(None, None, None, None, "strm"),
        P(None, None, None, None, "strm"),
        P("grp"),
        P("grp"),
    )
    out_specs = P(("grp", "strm"), None, "band", None, None)
    return jax.shard_map(body, mesh=mesh, in_specs=in_specs, out_specs=out_specs, check_vma=False)
```

```python
import jax
import jax.numpy as jnp
from jax import lax
from jax.experimental import pallas as pl
from jax.experimental.pallas import tpu as pltpu
from jax.sharding import PartitionSpec as P

epsilon = 1e-06
MESH = pl.DeviceIdType.MESH
F32 = jnp.float32
BF16 = jnp.bfloat16


def norm_silu(values, gain):
    mean_square = jnp.mean(values * values, axis=-1, keepdims=True)
    return jax.nn.silu(values * lax.rsqrt(mean_square + epsilon) * gain)


def dot_nk(left, right):
    return lax.dot_general(left, right, (((1,), (1,)), ((), ())), preferred_element_type=F32)


def kernel(
    slot_hbm, block_hbm, gain1_hbm, gain2_hbm, lat, c1, c2, w1, w2,
    out_ref, base_ref,
    LT, A1, KO, W1, W2, C, EA, XA, EB, XR, S, U, H, RB, Q,
    loc, s1, r1, s2, r2, sc, rc, sa, ra, se, re, su, ru, sw, rw, sq, rq,
    slot_ref, block_ref, gain1_ref, gain2_ref, gsem,
):
    p = lax.axis_index("strm")
    h = lax.axis_index("band")
    bands = lax.axis_size("band")
    core = lax.rem(p, 2)
    half = p // 2
    mate = p + 1 - 2 * core
    over = lax.rem(p + 2, 4)
    cross = lax.rem(mate + 2, 4)
    not_top = h > 0
    not_bottom = h < bands - 1

    def load(src, dst, i):
        copy = pltpu.make_async_copy(src, dst, loc.at[i])
        copy.start()
        return copy

    lat_copy = load(lat, LT, 0)
    smalls = [
        pltpu.make_async_copy(src, dst, gsem.at[i])
        for i, (src, dst) in enumerate(
            (
                (gain1_hbm, gain1_ref),
                (gain2_hbm, gain2_ref),
                (slot_hbm, slot_ref),
                (block_hbm, block_ref),
            )
        )
    ]
    for copy in smalls:
        copy.start()
    c1_copy = load(c1, KO.at[p], 1)

    barrier = pltpu.get_barrier_semaphore()
    for other in (mate, over, cross):
        pl.semaphore_signal(barrier, inc=1, device_id={"strm": other}, device_id_type=MESH)

    def greet(band):
        pl.semaphore_signal(barrier, inc=1, device_id={"band": band}, device_id_type=MESH)

    pl.when(not_top)(lambda: greet(h - 1))
    pl.when(not_bottom)(lambda: greet(h + 1))
    c2_copy = load(c2, C.at[p], 2)
    w1_copies = {j: load(w1.at[:, j], W1.at[j], 3 + j) for j in (2, 0, 1)}
    w2_copy = load(w2, W2.at[:, pl.ds(pl.multiple_of(48 * core, 16), 48)], 6)
    W2[:, 96:128] = jnp.zeros((27, 32, 192), BF16)

    @pl.when(h == 0)
    def _():
        XA[0] = jnp.zeros((2, 2, 16, 384), BF16)
        XR[0] = jnp.zeros((2, 2, 32, 128), BF16)

    @pl.when(h == bands - 1)
    def _():
        XA[1] = jnp.zeros((2, 2, 16, 384), BF16)
        XR[1] = jnp.zeros((2, 2, 32, 128), BF16)

    def cells(s):
        return pl.ds(pl.multiple_of(16 * s, 16), 16)

    for copy in smalls:
        copy.wait()
    gain1 = gain1_ref[...].reshape(1, 384)
    gain2 = gain2_ref[...].reshape(1, 192)
    lat_copy.wait()
    first_act = norm_silu(LT[...].astype(F32), gain1).astype(BF16)
    A1[2, cells(p)] = first_act[0:16]
    A1[3, cells(p)] = first_act[16:32]
    c1_copy.wait()

    peers = 3 + not_top.astype(jnp.int32) + not_bottom.astype(jnp.int32)
    pl.semaphore_wait(barrier, peers)

    def remote(src, dst, send, recv, strm, band):
        return pltpu.make_async_remote_copy(
            src_ref=src, dst_ref=dst, send_sem=send, recv_sem=recv,
            device_id={"strm": strm, "band": band}, device_id_type=MESH,
        )

    def kcopy(i, s, d):
        return remote(KO.at[s], KO.at[s], s2.at[i], r2.at[s], d, h)

    def acopy(i, s, d):
        rows = A1.at[2:4, cells(s)]
        return remote(rows, rows, s1.at[i], r1.at[s], d, h)

    def launch(copies):
        for copy in copies:
            copy.start()

    near = [make(i, p, d) for make in (kcopy, acopy) for i, d in enumerate((over, cross, mate))]
    launch(near)
    c2_copy.wait()
    c_over = remote(C.at[p], C.at[p], sc.at[0], rc.at[p], over, h)
    c_mate = remote(C.at[p], C.at[p], sc.at[1], rc.at[p], mate, h)
    c_over.start()
    c_mate.start()

    def carrive(s):
        remote(C.at[s], C.at[s], sc.at[0], rc.at[s], mate, h).wait_recv()

    for s in (mate, over, cross):
        kcopy(0, s, mate).wait_recv()
    for s in range(4):
        piece = KO[slot_ref[s]].astype(F32)
        piece = jnp.where(block_ref[s] > 0, piece, jnp.zeros_like(piece)).astype(BF16)
        for f in range(2):
            A1[f, 16 * s : 16 * s + 16] = piece[16 * f : 16 * f + 16]

    total = [[None] * 3 for _ in range(3)]

    def taps(j, i):
        rows = A1[i : i + 2].reshape(128, 384)
        for l in range(3):
            term = dot_nk(rows, W1[j, i, l])
            total[j][l] = term if total[j][l] is None else total[j][l] + term

    for j in (2, 0, 1):
        w1_copies[j].wait()
        taps(j, 0)

    for s in (mate, over, cross):
        acopy(0, s, mate).wait_recv()
    column = lax.rem(lax.broadcasted_iota(jnp.int32, (128, 192), 0), 16)

    def packed(j):
        taps(j, 1)
        taps(j, 2)
        full = (
            total[j][1]
            + jnp.where(column == 0, 0.0, pltpu.roll(total[j][0], 1, 0))
            + jnp.where(column == 15, 0.0, pltpu.roll(total[j][2], 127, 0))
        )
        rows = {}
        for k in range(2):
            for t in range(2):
                lo, hi = (
                    full[(t * 4 + k + n) * 16 : (t * 4 + k + n) * 16 + 16] for n in (0, 2)
                )
                rows[k, t] = jnp.concatenate(
                    [lo[:, 0:128], hi[:, 0:128], lo[:, 128:192], hi[:, 128:192]], axis=-1
                )
        return rows

    def offer(n, j):
        for (k, t), value in packed(j).items():
            EA[n, k, t] = value.astype(BF16)

    a_up = remote(EA.at[0], XA.at[1], sa.at[0], ra.at[1], p, h - 1)
    a_down = remote(EA.at[1], XA.at[0], sa.at[1], ra.at[0], p, h + 1)
    offer(0, 2)
    pl.when(not_top)(a_up.start)
    offer(1, 0)
    pl.when(not_bottom)(a_down.start)
    middle = packed(1)

    w2_copy.wait()

    def w2_rows(c):
        return W2.at[:, pl.ds(pl.multiple_of(48 * c, 16), 48)]

    w_mate = remote(w2_rows(core), w2_rows(core), sw, rw, mate, h)
    w_mate.start()
    carrive(over)
    c_fwd = remote(C.at[over], C.at[over], sc.at[2], rc.at[over], mate, h)
    c_fwd.start()

    def await_a(n):
        remote(EA.at[0], XA.at[n], sa.at[0], ra.at[n], mate, h).wait_recv()

    pl.when(not_top)(lambda: await_a(0))
    pl.when(not_bottom)(lambda: await_a(1))
    for (k, t), value in middle.items():
        S[k, t] = (value + XA[0, k, t].astype(F32) + XA[1, k, t].astype(F32)).astype(BF16)

    def ucopy(i, d):
        return remote(
            S.at[lax.rem(d, 2)], U.at[half, :, core], su.at[i], ru.at[half, core], d, h
        )

    u_own = [ucopy(i, d) for i, d in enumerate((over, cross, mate))]
    launch(u_own)
    U[half, :, core] = S[core]

    carrive(mate)
    carrive(cross)
    rows32 = lax.broadcasted_iota(jnp.int32, (32, 32), 0)
    cols32 = lax.broadcasted_iota(jnp.int32, (32, 32), 1)
    split = jnp.where(cols32 == 2 * lax.rem(rows32, 16) + rows32 // 16, 1.0, 0.0).astype(BF16)
    weave = jnp.where(rows32 == 2 * lax.rem(cols32, 16) + cols32 // 16, 1.0, 0.0).astype(BF16)

    for sp in range(2):
        s = core + 2 * sp
        chosen = C[slot_ref[s]]
        chosen = jnp.where(block_ref[s] > 0, chosen.astype(F32), 0.0).astype(BF16)
        for f in range(2):
            for row in range(2):
                moved = jnp.dot(split, chosen[f, row], preferred_element_type=F32).astype(BF16)
                H[f, row, sp * 32 : sp * 32 + 32] = moved
    remote(w2_rows(1 - core), w2_rows(1 - core), sw, rw, mate, h).wait_recv()
    def taps2(i, j, frames):
        n = len(frames)
        at = i * 9 + j * 3
        term = dot_nk(
            H[frames[0] : frames[0] + n].reshape(n * 128, 192), W2[at : at + 3].reshape(384, 192)
        )
        return term

    first = [[None] * 3 for _ in range(2)]
    for j in range(3):
        both = taps2(0, j, (0, 1))
        first[0][j] = both[0:128] + taps2(1, j, (1,))
        first[1][j] = both[128:256]

    def uarrive(b, a):
        remote(S.at[0], U.at[a, :, b], su.at[0], ru.at[a, b], mate, h).wait_recv()

    for b in range(2):
        for a in range(2):

            @pl.when(p != 2 * a + b)
            def _():
                uarrive(b, a)

    def advance(row):
        x = U[row].reshape(64, 384).astype(F32)
        parts = (
            jnp.concatenate([x[:, 0:128], x[:, 256:320]], axis=-1),
            jnp.concatenate([x[:, 128:256], x[:, 320:384]], axis=-1),
        )
        own = jnp.where(half == 0, parts[0], parts[1])
        for t in range(2):
            base_ref[t, row] = own[32 * t : 32 * t + 32]
        for sp in range(2):
            act = norm_silu(parts[sp], gain2).astype(BF16)
            for t in range(2):
                H[2 + t, row, sp * 32 : sp * 32 + 32] = act[32 * t : 32 * t + 32]

    advance(0)
    advance(1)

    def total2(j):
        both = taps2(2, j, (2, 3))
        return (first[0][j] + both[0:128], first[1][j] + both[128:256] + taps2(1, j, (2,)))

    def weave_columns(full):
        count = full.shape[0]
        y0, y1, y2 = full[:, 0:128], full[:, 128:256], full[:, 256:384]
        rows = lax.broadcasted_iota(jnp.int32, (count, 128), 0)
        even = lax.rem(rows // 16, 2) == 0
        place_w = lax.rem(rows, 16)
        before = jnp.where(
            even,
            jnp.where(place_w == 0, 0.0, pltpu.roll(y0, count - 15, 0)),
            pltpu.roll(y0, 16, 0),
        )
        after = jnp.where(
            even,
            pltpu.roll(y2, count - 16, 0),
            jnp.where(place_w == 15, 0.0, pltpu.roll(y2, 15, 0)),
        )
        return y1 + before + after

    def edge(n, totals):
        for t in range(2):
            result = weave_columns(totals[t][64 * n : 64 * n + 64]).astype(BF16)
            for sp in range(2):
                EB[n, sp, t] = result[32 * sp : 32 * sp + 32]

    def ecopies(n, band):
        return [
            remote(EB.at[n, sp], XR.at[1 - n, half], se.at[n, i], re.at[1 - n, half], d, band)
            for i, (sp, d) in enumerate(((1 - half, over), (half, p)))
        ]

    e_up = ecopies(0, h - 1)
    e_down = ecopies(1, h + 1)

    low_taps = total2(2)
    edge(0, low_taps)
    pl.when(not_top)(lambda: launch(e_up))
    high_taps = total2(0)
    edge(1, high_taps)
    pl.when(not_bottom)(lambda: launch(e_down))
    mid_taps = total2(1)
    mine = [[None] * 2 for _ in range(2)]
    for t in range(2):
        for a in range(2):
            other = low_taps[t][64:128] if a == 0 else high_taps[t][0:64]
            result = weave_columns(mid_taps[t][64 * a : 64 * a + 64] + other)
            for sp in range(2):
                RB[sp, t * 2 + a] = result[32 * sp : 32 * sp + 32].astype(BF16)
            mine[t][a] = jnp.where(half == 0, result[0:32], result[32:64])
    q = remote(RB.at[1 - half], Q, sq, rq, over, h)
    q.start()

    def earrive(n):
        for g in range(2):
            remote(EB.at[0, 0], XR.at[n, g], se.at[0, 0], re.at[n, g], over, h).wait_recv()

    pl.when(not_top)(lambda: earrive(0))
    pl.when(not_bottom)(lambda: earrive(1))
    q.wait_recv()
    for t in range(2):
        for a in range(2):
            theirs = Q[t * 2 + a].astype(F32)
            low = jnp.where(half == 0, mine[t][a], theirs) + XR[a, 0, t].astype(F32)
            high = jnp.where(half == 0, theirs, mine[t][a]) + XR[a, 1, t].astype(F32)
            branch = jnp.concatenate([low[:, 0:96], high[:, 0:96]], axis=-1).astype(BF16)
            total_ta = (base_ref[t, a] + branch.astype(F32)).astype(BF16)
            out_ref[t, a] = jnp.dot(weave, total_ta, preferred_element_type=F32).astype(BF16)

    q.wait_send()
    for copy in (*near, c_over, c_mate, c_fwd, w_mate, *u_own):
        copy.wait_send()

    def left(rows):
        for row in rows:
            row.wait_send()

    pl.when(not_top)(lambda: left([a_up] + e_up))
    pl.when(not_bottom)(lambda: left([a_down] + e_down))


def hbm(x):
    return pltpu.with_memory_space_constraint(x, pltpu.HBM)


def body(
    latents, cache_first, cache_second, gain_first, gain_second, w_first, w_second,
    cache_slot, block_index,
):
    any_spec = pl.BlockSpec(memory_space=pltpu.HBM)
    vmem = pl.BlockSpec(memory_space=pltpu.VMEM)
    smem = pl.BlockSpec(memory_space=pltpu.SMEM)
    dma = pltpu.SemaphoreType.DMA
    decoded = pl.pallas_call(
        kernel,
        out_shape=jax.ShapeDtypeStruct((2, 2, 32, 192), BF16),
        in_specs=[any_spec] * 9,
        out_specs=vmem,
        scratch_shapes=[
            pltpu.VMEM((2, 2, 32, 192), F32),
            pltpu.VMEM((32, 384), BF16),
            pltpu.VMEM((4, 64, 384), BF16),
            pltpu.VMEM((4, 32, 384), BF16),
            pltpu.VMEM((3, 3, 3, 192, 384), BF16),
            pltpu.VMEM((27, 128, 192), BF16),
            pltpu.VMEM((4, 2, 2, 32, 192), BF16),
            pltpu.VMEM((2, 2, 2, 16, 384), BF16),
            pltpu.VMEM((2, 2, 2, 16, 384), BF16),
            pltpu.VMEM((2, 2, 2, 32, 128), BF16),
            pltpu.VMEM((2, 2, 2, 32, 128), BF16),
            pltpu.VMEM((2, 2, 16, 384), BF16),
            pltpu.VMEM((2, 2, 2, 16, 384), BF16),
            pltpu.VMEM((4, 2, 64, 192), BF16),
            pltpu.VMEM((2, 4, 32, 128), BF16),
            pltpu.VMEM((4, 32, 128), BF16),
            dma((7,)),
            dma((3,)),
            dma((4,)),
            dma((3,)),
            dma((4,)),
            dma((3,)),
            dma((4,)),
            dma((2,)),
            dma((2,)),
            dma((2, 2)),
            dma((2, 2)),
            dma((3,)),
            dma((2, 2)),
            dma,
            dma,
            dma,
            dma,
            pltpu.SMEM((4,), jnp.int32),
            pltpu.SMEM((4,), jnp.int32),
            pltpu.VMEM((384,), F32),
            pltpu.VMEM((192,), F32),
            dma((4,)),
        ],
        compiler_params=pltpu.CompilerParams(
            collective_id=0, has_side_effects=True, vmem_limit_bytes=40 * 1024 * 1024
        ),
    )(
        hbm(cache_slot),
        hbm(block_index),
        hbm(gain_first),
        hbm(gain_second),
        hbm(latents.reshape(32, 384)),
        hbm(cache_first.reshape(32, 384)),
        hbm(cache_second.reshape(2, 2, 32, 192)),
        hbm(w_first.transpose(0, 1, 2, 4, 3)),
        hbm(w_second.transpose(0, 1, 2, 4, 3).reshape(27, 48, 192)),
    )
    return decoded.reshape(1, 2, 2, 32, 192)


def solution(mesh):
    in_specs = (
        P(("grp", "strm"), None, "band", None, None),
        P(("grp", "strm"), None, "band", None, None),
        P(("grp", "strm"), None, "band", None, None),
        P(),
        P(),
        P(None, None, None, None, "strm"),
        P(None, None, None, None, "strm"),
        P("grp"),
        P("grp"),
    )
    out_specs = P(("grp", "strm"), None, "band", None, None)
    return jax.shard_map(body, mesh=mesh, in_specs=in_specs, out_specs=out_specs, check_vma=False)
```

```python
import jax
import jax.numpy as jnp
from jax import lax
from jax.experimental import pallas as pl
from jax.experimental.pallas import tpu as pltpu
from jax.sharding import PartitionSpec as P

epsilon = 1e-06
MESH = pl.DeviceIdType.MESH
F32 = jnp.float32
BF16 = jnp.bfloat16


def norm_silu(values, gain):
    mean_square = jnp.mean(values * values, axis=-1, keepdims=True)
    return jax.nn.silu(values * lax.rsqrt(mean_square + epsilon) * gain)


def dot_nk(left, right):
    return lax.dot_general(left, right, (((1,), (1,)), ((), ())), preferred_element_type=F32)


def kernel(
    slot_hbm, block_hbm, gain1_hbm, gain2_hbm, lat, c1, c2, w1, w2,
    out_ref, base_ref,
    LT, A1, KO, WA, WB, T, W2, C, EA, XA, EB, XR, S, U, H, RB, Q,
    loc, s1, r1, s2, r2, sc, rc, sa, ra, se, re, su, ru, sw, rw, sq, rq,
    slot_ref, block_ref, gain1_ref, gain2_ref, gsem,
):
    p = lax.axis_index("strm")
    h = lax.axis_index("band")
    bands = lax.axis_size("band")
    core = lax.rem(p, 2)
    half = p // 2
    mate = p + 1 - 2 * core
    over = lax.rem(p + 2, 4)
    cross = lax.rem(mate + 2, 4)
    not_top = h > 0
    not_bottom = h < bands - 1

    def load(src, dst, i):
        copy = pltpu.make_async_copy(src, dst, loc.at[i])
        copy.start()
        return copy

    lat_copy = load(lat, LT, 0)
    smalls = [
        pltpu.make_async_copy(src, dst, gsem.at[i])
        for i, (src, dst) in enumerate(
            (
                (gain1_hbm, gain1_ref),
                (gain2_hbm, gain2_ref),
                (slot_hbm, slot_ref),
                (block_hbm, block_ref),
            )
        )
    ]
    for copy in smalls:
        copy.start()
    c1_copy = load(c1, KO.at[p], 1)

    barrier = pltpu.get_barrier_semaphore()
    for other in (mate, over, cross):
        pl.semaphore_signal(barrier, inc=1, device_id={"strm": other}, device_id_type=MESH)

    def greet(band):
        pl.semaphore_signal(barrier, inc=1, device_id={"band": band}, device_id_type=MESH)

    pl.when(not_top)(lambda: greet(h - 1))
    pl.when(not_bottom)(lambda: greet(h + 1))
    c2_copy = load(c2, C.at[p], 2)
    w1_copies = (
        load(w1.at[0], WA, 3),
        load(w1.at[1], WB.at[:, :, :, pl.ds(0, 384)], 4),
        load(w1.at[2], WB.at[:, :, :, pl.ds(384, 384)], 5),
    )
    w2_copy = load(w2, W2.at[:, pl.ds(pl.multiple_of(48 * core, 16), 48)], 6)
    W2[:, 96:128] = jnp.zeros((27, 32, 192), BF16)

    @pl.when(h == 0)
    def _():
        XA[0] = jnp.zeros((2, 2, 16, 384), BF16)
        XR[0] = jnp.zeros((2, 2, 32, 128), BF16)

    @pl.when(h == bands - 1)
    def _():
        XA[1] = jnp.zeros((2, 2, 16, 384), BF16)
        XR[1] = jnp.zeros((2, 2, 32, 128), BF16)

    def cells(s):
        return pl.ds(pl.multiple_of(16 * s, 16), 16)

    for copy in smalls:
        copy.wait()
    gain1 = gain1_ref[...].reshape(1, 384)
    gain2 = gain2_ref[...].reshape(1, 192)
    lat_copy.wait()
    first_act = norm_silu(LT[...].astype(F32), gain1).astype(BF16)
    A1[2, cells(p)] = first_act[0:16]
    A1[3, cells(p)] = first_act[16:32]
    c1_copy.wait()

    peers = 3 + not_top.astype(jnp.int32) + not_bottom.astype(jnp.int32)
    pl.semaphore_wait(barrier, peers)

    def remote(src, dst, send, recv, strm, band):
        return pltpu.make_async_remote_copy(
            src_ref=src, dst_ref=dst, send_sem=send, recv_sem=recv,
            device_id={"strm": strm, "band": band}, device_id_type=MESH,
        )

    def kcopy(i, s, d):
        return remote(KO.at[s], KO.at[s], s2.at[i], r2.at[s], d, h)

    def acopy(i, s, d):
        rows = A1.at[2:4, cells(s)]
        return remote(rows, rows, s1.at[i], r1.at[s], d, h)

    def launch(copies):
        for copy in copies:
            copy.start()

    near = [make(i, p, d) for make in (kcopy, acopy) for i, d in enumerate((over, cross, mate))]
    launch(near)
    c2_copy.wait()
    c_over = remote(C.at[p], C.at[p], sc.at[0], rc.at[p], over, h)
    c_mate = remote(C.at[p], C.at[p], sc.at[1], rc.at[p], mate, h)
    c_over.start()
    c_mate.start()

    def carrive(s):
        remote(C.at[s], C.at[s], sc.at[0], rc.at[s], mate, h).wait_recv()

    for s in (mate, over, cross):
        kcopy(0, s, mate).wait_recv()
    for s in range(4):
        piece = KO[slot_ref[s]].astype(F32)
        piece = jnp.where(block_ref[s] > 0, piece, jnp.zeros_like(piece)).astype(BF16)
        for f in range(2):
            A1[f, 16 * s : 16 * s + 16] = piece[16 * f : 16 * f + 16]

    w1_copies[0].wait()
    cached = A1[0:2].reshape(128, 384)
    for j in (2, 0, 1):
        for l in range(3):
            T[j, l] = dot_nk(cached, WA[j, l])
    w1_copies[1].wait()
    w1_copies[2].wait()

    for s in (mate, over, cross):
        acopy(0, s, mate).wait_recv()
    recent = jnp.concatenate(
        [A1[1:3].reshape(128, 384), A1[2:4].reshape(128, 384)], axis=-1
    )
    column = lax.rem(lax.broadcasted_iota(jnp.int32, (128, 192), 0), 16)

    def packed(j):
        total = [T[j, l] + dot_nk(recent, WB[j, l]) for l in range(3)]
        full = (
            total[1]
            + jnp.where(column == 0, 0.0, pltpu.roll(total[0], 1, 0))
            + jnp.where(column == 15, 0.0, pltpu.roll(total[2], 127, 0))
        )
        rows = {}
        for k in range(2):
            for t in range(2):
                lo, hi = (
                    full[(t * 4 + k + n) * 16 : (t * 4 + k + n) * 16 + 16] for n in (0, 2)
                )
                rows[k, t] = jnp.concatenate(
                    [lo[:, 0:128], hi[:, 0:128], lo[:, 128:192], hi[:, 128:192]], axis=-1
                )
        return rows

    def offer(n, j):
        for (k, t), value in packed(j).items():
            EA[n, k, t] = value.astype(BF16)

    a_up = remote(EA.at[0], XA.at[1], sa.at[0], ra.at[1], p, h - 1)
    a_down = remote(EA.at[1], XA.at[0], sa.at[1], ra.at[0], p, h + 1)
    offer(0, 2)
    pl.when(not_top)(a_up.start)
    offer(1, 0)
    pl.when(not_bottom)(a_down.start)
    middle = packed(1)

    w2_copy.wait()

    def w2_rows(c):
        return W2.at[:, pl.ds(pl.multiple_of(48 * c, 16), 48)]

    w_mate = remote(w2_rows(core), w2_rows(core), sw, rw, mate, h)
    w_mate.start()
    carrive(over)
    c_fwd = remote(C.at[over], C.at[over], sc.at[2], rc.at[over], mate, h)
    c_fwd.start()

    def await_a(n):
        remote(EA.at[0], XA.at[n], sa.at[0], ra.at[n], mate, h).wait_recv()

    pl.when(not_top)(lambda: await_a(0))
    pl.when(not_bottom)(lambda: await_a(1))
    for (k, t), value in middle.items():
        S[k, t] = (value + XA[0, k, t].astype(F32) + XA[1, k, t].astype(F32)).astype(BF16)

    def ucopy(i, d):
        return remote(
            S.at[lax.rem(d, 2)], U.at[half, :, core], su.at[i], ru.at[half, core], d, h
        )

    u_own = [ucopy(i, d) for i, d in enumerate((over, cross, mate))]
    launch(u_own)
    U[half, :, core] = S[core]

    carrive(mate)
    carrive(cross)
    rows32 = lax.broadcasted_iota(jnp.int32, (32, 32), 0)
    cols32 = lax.broadcasted_iota(jnp.int32, (32, 32), 1)
    split = jnp.where(cols32 == 2 * lax.rem(rows32, 16) + rows32 // 16, 1.0, 0.0).astype(BF16)
    weave = jnp.where(rows32 == 2 * lax.rem(cols32, 16) + cols32 // 16, 1.0, 0.0).astype(BF16)

    for sp in range(2):
        s = core + 2 * sp
        chosen = C[slot_ref[s]]
        chosen = jnp.where(block_ref[s] > 0, chosen.astype(F32), 0.0).astype(BF16)
        for f in range(2):
            for row in range(2):
                moved = jnp.dot(split, chosen[f, row], preferred_element_type=F32).astype(BF16)
                H[f, row, sp * 32 : sp * 32 + 32] = moved
    remote(w2_rows(1 - core), w2_rows(1 - core), sw, rw, mate, h).wait_recv()
    def taps2(i, j, frames):
        n = len(frames)
        at = i * 9 + j * 3
        term = dot_nk(
            H[frames[0] : frames[0] + n].reshape(n * 128, 192), W2[at : at + 3].reshape(384, 192)
        )
        return term

    first = [[None] * 3 for _ in range(2)]
    for j in range(3):
        both = taps2(0, j, (0, 1))
        first[0][j] = both[0:128] + taps2(1, j, (1,))
        first[1][j] = both[128:256]

    def uarrive(b, a):
        remote(S.at[0], U.at[a, :, b], su.at[0], ru.at[a, b], mate, h).wait_recv()

    for b in range(2):
        for a in range(2):

            @pl.when(p != 2 * a + b)
            def _():
                uarrive(b, a)

    def advance(row):
        x = U[row].reshape(64, 384).astype(F32)
        parts = (
            jnp.concatenate([x[:, 0:128], x[:, 256:320]], axis=-1),
            jnp.concatenate([x[:, 128:256], x[:, 320:384]], axis=-1),
        )
        own = jnp.where(half == 0, parts[0], parts[1])
        for t in range(2):
            base_ref[t, row] = own[32 * t : 32 * t + 32]
        for sp in range(2):
            act = norm_silu(parts[sp], gain2).astype(BF16)
            for t in range(2):
                H[2 + t, row, sp * 32 : sp * 32 + 32] = act[32 * t : 32 * t + 32]

    advance(0)
    advance(1)

    def total2(j):
        both = taps2(2, j, (2, 3))
        return (first[0][j] + both[0:128], first[1][j] + both[128:256] + taps2(1, j, (2,)))

    def weave_columns(full):
        count = full.shape[0]
        y0, y1, y2 = full[:, 0:128], full[:, 128:256], full[:, 256:384]
        rows = lax.broadcasted_iota(jnp.int32, (count, 128), 0)
        even = lax.rem(rows // 16, 2) == 0
        place_w = lax.rem(rows, 16)
        before = jnp.where(
            even,
            jnp.where(place_w == 0, 0.0, pltpu.roll(y0, count - 15, 0)),
            pltpu.roll(y0, 16, 0),
        )
        after = jnp.where(
            even,
            pltpu.roll(y2, count - 16, 0),
            jnp.where(place_w == 15, 0.0, pltpu.roll(y2, 15, 0)),
        )
        return y1 + before + after

    def edge(n, totals):
        for t in range(2):
            result = weave_columns(totals[t][64 * n : 64 * n + 64]).astype(BF16)
            for sp in range(2):
                EB[n, sp, t] = result[32 * sp : 32 * sp + 32]

    def ecopies(n, band):
        return [
            remote(EB.at[n, sp], XR.at[1 - n, half], se.at[n, i], re.at[1 - n, half], d, band)
            for i, (sp, d) in enumerate(((1 - half, over), (half, p)))
        ]

    e_up = ecopies(0, h - 1)
    e_down = ecopies(1, h + 1)

    low_taps = total2(2)
    edge(0, low_taps)
    pl.when(not_top)(lambda: launch(e_up))
    high_taps = total2(0)
    edge(1, high_taps)
    pl.when(not_bottom)(lambda: launch(e_down))
    mid_taps = total2(1)
    mine = [[None] * 2 for _ in range(2)]
    for t in range(2):
        for a in range(2):
            other = low_taps[t][64:128] if a == 0 else high_taps[t][0:64]
            result = weave_columns(mid_taps[t][64 * a : 64 * a + 64] + other)
            for sp in range(2):
                RB[sp, t * 2 + a] = result[32 * sp : 32 * sp + 32].astype(BF16)
            mine[t][a] = jnp.where(half == 0, result[0:32], result[32:64])
    q = remote(RB.at[1 - half], Q, sq, rq, over, h)
    q.start()

    def earrive(n):
        for g in range(2):
            remote(EB.at[0, 0], XR.at[n, g], se.at[0, 0], re.at[n, g], over, h).wait_recv()

    pl.when(not_top)(lambda: earrive(0))
    pl.when(not_bottom)(lambda: earrive(1))
    q.wait_recv()
    for t in range(2):
        for a in range(2):
            theirs = Q[t * 2 + a].astype(F32)
            low = jnp.where(half == 0, mine[t][a], theirs) + XR[a, 0, t].astype(F32)
            high = jnp.where(half == 0, theirs, mine[t][a]) + XR[a, 1, t].astype(F32)
            branch = jnp.concatenate([low[:, 0:96], high[:, 0:96]], axis=-1).astype(BF16)
            total_ta = (base_ref[t, a] + branch.astype(F32)).astype(BF16)
            out_ref[t, a] = jnp.dot(weave, total_ta, preferred_element_type=F32).astype(BF16)

    q.wait_send()
    for copy in (*near, c_over, c_mate, c_fwd, w_mate, *u_own):
        copy.wait_send()

    def left(rows):
        for row in rows:
            row.wait_send()

    pl.when(not_top)(lambda: left([a_up] + e_up))
    pl.when(not_bottom)(lambda: left([a_down] + e_down))


def hbm(x):
    return pltpu.with_memory_space_constraint(x, pltpu.HBM)


def body(
    latents, cache_first, cache_second, gain_first, gain_second, w_first, w_second,
    cache_slot, block_index,
):
    any_spec = pl.BlockSpec(memory_space=pltpu.HBM)
    vmem = pl.BlockSpec(memory_space=pltpu.VMEM)
    smem = pl.BlockSpec(memory_space=pltpu.SMEM)
    dma = pltpu.SemaphoreType.DMA
    decoded = pl.pallas_call(
        kernel,
        out_shape=jax.ShapeDtypeStruct((2, 2, 32, 192), BF16),
        in_specs=[any_spec] * 9,
        out_specs=vmem,
        scratch_shapes=[
            pltpu.VMEM((2, 2, 32, 192), F32),
            pltpu.VMEM((32, 384), BF16),
            pltpu.VMEM((4, 64, 384), BF16),
            pltpu.VMEM((4, 32, 384), BF16),
            pltpu.VMEM((3, 3, 192, 384), BF16),
            pltpu.VMEM((3, 3, 192, 768), BF16),
            pltpu.VMEM((3, 3, 128, 192), F32),
            pltpu.VMEM((27, 128, 192), BF16),
            pltpu.VMEM((4, 2, 2, 32, 192), BF16),
            pltpu.VMEM((2, 2, 2, 16, 384), BF16),
            pltpu.VMEM((2, 2, 2, 16, 384), BF16),
            pltpu.VMEM((2, 2, 2, 32, 128), BF16),
            pltpu.VMEM((2, 2, 2, 32, 128), BF16),
            pltpu.VMEM((2, 2, 16, 384), BF16),
            pltpu.VMEM((2, 2, 2, 16, 384), BF16),
            pltpu.VMEM((4, 2, 64, 192), BF16),
            pltpu.VMEM((2, 4, 32, 128), BF16),
            pltpu.VMEM((4, 32, 128), BF16),
            dma((7,)),
            dma((3,)),
            dma((4,)),
            dma((3,)),
            dma((4,)),
            dma((3,)),
            dma((4,)),
            dma((2,)),
            dma((2,)),
            dma((2, 2)),
            dma((2, 2)),
            dma((3,)),
            dma((2, 2)),
            dma,
            dma,
            dma,
            dma,
            pltpu.SMEM((4,), jnp.int32),
            pltpu.SMEM((4,), jnp.int32),
            pltpu.VMEM((384,), F32),
            pltpu.VMEM((192,), F32),
            dma((4,)),
        ],
        compiler_params=pltpu.CompilerParams(
            collective_id=0, has_side_effects=True, vmem_limit_bytes=40 * 1024 * 1024
        ),
    )(
        hbm(cache_slot),
        hbm(block_index),
        hbm(gain_first),
        hbm(gain_second),
        hbm(latents.reshape(32, 384)),
        hbm(cache_first.reshape(32, 384)),
        hbm(cache_second.reshape(2, 2, 32, 192)),
        hbm(w_first.transpose(0, 1, 2, 4, 3)),
        hbm(w_second.transpose(0, 1, 2, 4, 3).reshape(27, 48, 192)),
    )
    return decoded.reshape(1, 2, 2, 32, 192)


def solution(mesh):
    in_specs = (
        P(("grp", "strm"), None, "band", None, None),
        P(("grp", "strm"), None, "band", None, None),
        P(("grp", "strm"), None, "band", None, None),
        P(),
        P(),
        P(None, None, None, None, "strm"),
        P(None, None, None, None, "strm"),
        P("grp"),
        P("grp"),
    )
    out_specs = P(("grp", "strm"), None, "band", None, None)
    return jax.shard_map(body, mesh=mesh, in_specs=in_specs, out_specs=out_specs, check_vma=False)
```
